32 devices in a mesh: groups: 2 (over y), blk: 4 (over z), split: 2 (over x), sub: 2 (over core).
Axes of the slice: x: 2, y: 2, z: 4, core: 2. Of those that a mesh axis runs over, the one named last changes fastest.
Arguments:
- attention_output_rows: bfloat16 [1024, 8192], P(('groups', 'blk'), 'split'), parts along dimension 0, may hold values from -6 to 6
- residual: bfloat16 [1024, 8192], P(('groups', 'split'), ('blk', 'sub')), parts along dimension 0, may hold values from -6 to 6
- output_projection_weight: bfloat16 [8192, 8192], P('split', ('blk', 'sub')), may hold values from -0.0625 to 0.0625
- down_adapter_bank: bfloat16 [4, 64, 8192], P('blk', None, 'split'), may hold values from -0.0625 to 0.0625
- up_adapter_bank: bfloat16 [4, 64, 8192], P('split', None, ('blk', 'sub')), may hold values from -0.75 to 0.75
- rollout_row_tenant: int32 [1024], P('groups'), parts along dimension 0, may hold values from 0 to 3, as said below
- tenant_bank_entry: int32 [4], replicated, may hold values from 0 to 3, each once
- tenant_live_rank: int32 [4], replicated, may hold values from 16 to 64, as said below
Outputs:
- layer_out: bfloat16 [1024, 8192], P(('groups', 'split'), ('blk', 'sub')), parts along dimension 0
The draws below stay inside these ranges and needn't reach their ends.
There are 2 independent parts, one for each index of `groups`. The reference program is written for one: setup_inputs(seed, part) draws one part's arguments, and reference() takes and returns one part's arrays. A program takes and returns all parts, laid end to end along the dimension named above; an argument that names none is the same for every part. Nothing has to cross between parts.
Inputs may be any that keep to these rules, and one draw needn't show every extreme that they name: `rollout_row_tenant`: every tenant owns at least one row of every part. `tenant_live_rank`: some tenant has the full rank 64.
All inputs are finite; a program needn't handle non-finite values.
Results may differ from the reference program's by a relative error of at most 0.0038.
Values may be sent and summed in bfloat16 or wider, within the bound.
A program may use at most 64 MiB of HBM per device.

```python
import jax
import jax.numpy as jnp

MODEL_WIDTH = 8192
PADDED_RANK = 64
TOKENS = 512
TENANT_TOTAL = 4


def draw_rollout_row_tenant(key, part):
    first_key, second_key, order_key, mix_key = jax.random.split(jax.random.fold_in(key, 11), 4)
    first = jax.random.randint(first_key, (TOKENS,), 0, TENANT_TOTAL)
    second = jax.random.randint(second_key, (TOKENS,), 0, TENANT_TOTAL)
    skewed = jnp.minimum(first, second)
    order = jax.random.permutation(order_key, TENANT_TOTAL)
    tenant_ids = order[skewed].astype(jnp.int32)
    tenant_ids = tenant_ids.at[:TENANT_TOTAL].set(jnp.arange(TENANT_TOTAL, dtype=jnp.int32))
    return jax.random.permutation(mix_key, tenant_ids).astype(jnp.int32)


def draw_tenant_live_rank(key, part):
    value_key, place_key = jax.random.split(jax.random.fold_in(key, 23), 2)
    ranks = jax.random.randint(value_key, (TENANT_TOTAL,), PADDED_RANK // 4, PADDED_RANK + 1)
    position = jax.random.randint(place_key, (), 0, TENANT_TOTAL)
    return ranks.at[position].set(PADDED_RANK).astype(jnp.int32)


def levels(own_key, extent, shards, smallest, largest):
    loudness = 1.0
    for dim, blocks in shards:
        heights = jax.random.uniform(jax.random.fold_in(jax.random.fold_in(own_key, 6), dim), (blocks,), jnp.float32, smallest / len(shards), largest / len(shards))
        loudness = loudness * jnp.repeat(jnp.exp(heights), extent[dim] // blocks).reshape((-1,) + (1,) * (len(extent) - 1 - dim))
    return loudness


def noise(key, dims, width, reach, pieces=(), held_as=jnp.bfloat16):
    values = width * jax.random.normal(key, dims, jnp.float32)
    if pieces:
        values = values * levels(key, dims, pieces, -0.22, 0.18)
    return jnp.clip(values, -reach, reach).astype(held_as)


def setup_inputs(seed: int = 0, part: int = 0) -> dict:
    keys = jax.random.split(jax.random.key(seed), 9)
    part_keys = jax.random.split(jax.random.fold_in(keys[8], part), 9)
    return {
        "attention_output_rows": noise(part_keys[0], (TOKENS, MODEL_WIDTH), 1.0, 6.0, ((0, 4), (1, 2))),
        "residual": noise(part_keys[1], (TOKENS, MODEL_WIDTH), 1.0, 6.0, ((0, 2), (1, 8))),
        "output_projection_weight": noise(keys[2], (MODEL_WIDTH, MODEL_WIDTH), MODEL_WIDTH ** -0.5, 0.0625, ((0, 2), (1, 8))),
        "down_adapter_bank": noise(keys[3], (TENANT_TOTAL, PADDED_RANK, MODEL_WIDTH), MODEL_WIDTH ** -0.5, 0.0625, ((0, 4), (2, 2))),
        "up_adapter_bank": noise(keys[4], (TENANT_TOTAL, PADDED_RANK, MODEL_WIDTH), PADDED_RANK ** -0.5, 0.75, ((0, 2), (2, 8))),
        "rollout_row_tenant": draw_rollout_row_tenant(jax.random.fold_in(jax.random.fold_in(keys[8], part), 71), part),
        "tenant_bank_entry": jax.random.permutation(keys[6], TENANT_TOTAL).astype(jnp.int32),
        "tenant_live_rank": draw_tenant_live_rank(jax.random.fold_in(keys[8], 71), part),
    }


def reference(attention_output_rows, residual, output_projection_weight, down_adapter_bank, up_adapter_bank, rollout_row_tenant, tenant_bank_entry, tenant_live_rank):
    frozen_output_term = jnp.dot(attention_output_rows, output_projection_weight, preferred_element_type=jnp.float32)
    slot_row = tenant_bank_entry[rollout_row_tenant]
    rank_row = tenant_live_rank[rollout_row_tenant]
    reduced_rank_rows = jnp.dot(attention_output_rows, down_adapter_bank.reshape(TENANT_TOTAL * PADDED_RANK, MODEL_WIDTH).T, preferred_element_type=jnp.float32)
    low_rank = jnp.take_along_axis(reduced_rank_rows.reshape(TOKENS, TENANT_TOTAL, PADDED_RANK), slot_row[:, None, None], axis=1)[:, 0, :]
    kept_mask = jnp.arange(PADDED_RANK)[None, :] < rank_row[:, None]
    scaling = PADDED_RANK / rank_row.astype(jnp.float32)
    low_scaled = jnp.where(kept_mask, low_rank * scaling[:, None], 0.0).astype(jnp.bfloat16)
    slot_hot = slot_row[:, None] == jnp.arange(TENANT_TOTAL)[None, :]
    rank_expanded_rows = jnp.where(slot_hot[:, :, None], low_scaled[:, None, :], jnp.zeros((), jnp.bfloat16)).reshape(TOKENS, TENANT_TOTAL * PADDED_RANK)
    adapter_output_term = jnp.dot(rank_expanded_rows, up_adapter_bank.reshape(TENANT_TOTAL * PADDED_RANK, MODEL_WIDTH), preferred_element_type=jnp.float32)
    return (residual.astype(jnp.float32) + frozen_output_term + adapter_output_term).astype(jnp.bfloat16)
```

```python
import functools

import jax
import jax.numpy as jnp
from jax import lax
from jax.experimental import pallas as pl
from jax.experimental.pallas import tpu as pltpu
from jax.sharding import PartitionSpec as P

CHUNK_ROWS = 32
MESH = pl.DeviceIdType.MESH


def kernel(
    nb, ns, nu, rc,
    ent_ref, rank_ref, x_ref, r_ref, w_ref, dn_ref, up_ref, ten_ref, o_ref,
    xall, wv, rv, dnp, upp, mtab, acc, lacc, xs, ls, xr, lr, lowx,
    sem_loc, sem_own, zsend, zrecv, csend, crecv, usend, urecv,
    xsend, xrecv, lsend, lrecv, gsend, grecv,
):
    blk, split, sub = lax.axis_index("blk"), lax.axis_index("split"), lax.axis_index("sub")
    rows, feats = x_ref.shape
    cols = w_ref.shape[1]
    own = r_ref.shape[0]
    banks, rank = dn_ref.shape[0], dn_ref.shape[1]
    up_banks = up_ref.shape[0]
    wide = dnp.shape[0]
    total = ten_ref.shape[1]
    tenants = ent_ref.shape[0]
    nc = rows // rc
    half = rc // nu

    w_copy = pltpu.make_async_copy(w_ref, wv, sem_loc.at[0])
    w_copy.start()
    x_copy = pltpu.make_async_copy(
        x_ref, xall.at[pl.ds(pl.multiple_of(blk * rows, rows), rows)], sem_own
    )
    x_copy.start()
    loads = [pltpu.make_async_copy(r_ref, rv, sem_loc.at[1])]
    for e in range(banks):
        loads.append(
            pltpu.make_async_copy(dn_ref.at[e], dnp.at[pl.ds(e * rank, rank)], sem_loc.at[2 + e])
        )

    def up_slot(bank):
        return upp.at[bank // banks, pl.ds(pl.multiple_of(bank % banks * rank, rank), rank)]

    for e in range(up_banks):
        loads.append(
            pltpu.make_async_copy(
                up_ref.at[e], up_slot(split * up_banks + e), sem_loc.at[2 + banks + e]
            )
        )
    for load in loads:
        load.start()

    barrier = pltpu.get_barrier_semaphore()
    for k in range(1, nb):
        pl.semaphore_signal(
            barrier, inc=1, device_id={"blk": lax.rem(blk + k, nb)}, device_id_type=MESH
        )
    for k in range(1, ns):
        pl.semaphore_signal(
            barrier, inc=1, device_id={"split": lax.rem(split + k, ns)}, device_id_type=MESH
        )
    for k in range(1, nu):
        pl.semaphore_signal(
            barrier, inc=1, device_id={"sub": lax.rem(sub + k, nu)}, device_id_type=MESH
        )
    pl.semaphore_wait(barrier, nb + ns + nu - 3)

    def half_rows(ref, b, j, core):
        start = pl.multiple_of(b * rows + j * rc + core * half, half)
        return ref.at[pl.ds(start, half)]

    def z_copy(b, j, side, src=None):
        dst = half_rows(xall, b, j, sub)
        return pltpu.make_async_remote_copy(
            src_ref=dst if src is None else src,
            dst_ref=dst,
            send_sem=zsend.at[side, b * nc + j],
            recv_sem=zrecv.at[b * nc + j],
            device_id={"blk": lax.rem(blk + 1 - 2 * side + nb, nb)},
            device_id_type=MESH,
        )

    def c_copy(b, j, k, core):
        piece = half_rows(xall, b, j, core)
        return pltpu.make_async_remote_copy(
            src_ref=piece,
            dst_ref=piece,
            send_sem=csend.at[k - 1, b * nc + j],
            recv_sem=crecv.at[k - 1, b * nc + j],
            device_id={"sub": lax.rem(sub + k, nu)},
            device_id_type=MESH,
        )

    for j in range(nc):
        src = x_ref.at[pl.ds(pl.multiple_of(j * rc + sub * half, half), half)]

        @pl.when(blk < nb - 1)
        def _():
            z_copy(blk, j, 0, src).start()

        @pl.when(blk > 0)
        def _():
            z_copy(blk, j, 1, src).start()

    def u_copy(k, e, owner):
        return pltpu.make_async_remote_copy(
            src_ref=up_ref.at[e],
            dst_ref=up_slot(owner * up_banks + e),
            send_sem=usend.at[k - 1, e],
            recv_sem=urecv.at[k - 1, e],
            device_id={"split": lax.rem(split + k, ns)},
            device_id_type=MESH,
        )

    for k in range(1, ns):
        for e in range(up_banks):
            u_copy(k, e, split).start()

    if wide > banks * rank:
        pad = wide - banks * rank
        dnp[pl.ds(banks * rank, pad), :] = jnp.zeros((pad, feats), dnp.dtype)
        for p in range(nb):
            upp[p, pl.ds(banks * rank, pad), :] = jnp.zeros((pad, cols), upp.dtype)
    lane = lax.broadcasted_iota(jnp.int32, (1, wide), 1)
    tcol = jnp.transpose(
        jnp.broadcast_to(ten_ref[...].astype(jnp.float32), (8, total))
    )[:, :1]
    table = jnp.zeros((total, wide), jnp.float32)
    for t in range(tenants):
        live = jnp.full((1, wide), rank_ref[t], jnp.int32)
        slot = jnp.full((1, wide), ent_ref[t], jnp.int32)
        line = jnp.zeros((1, wide), jnp.float32)
        for e in range(banks):
            keep = (
                (lane >= e * rank) & (lane < e * rank + jnp.minimum(live, rank))
                & (slot == blk * banks + e)
            )
            line = jnp.where(keep, rank / live.astype(jnp.float32), line)
        table = jnp.where(tcol == t, line, table)
    mtab[...] = table

    for load in loads:
        load.wait()
    x_copy.wait()
    w_copy.wait()

    def x_pair(xo, b, j, src_split, count=2):
        start = pl.multiple_of(b * rows + j * rc, rc)
        dest = pl.multiple_of(b * rows + j * rc - xo * own, rc)
        chunk, mine = b * nc + j, (b * rows + j * rc - xo * own) // rc
        pairs = ((ls, lr, lsend, lrecv), (xs, xr, xsend, xrecv))
        return [
            pltpu.make_async_remote_copy(
                src_ref=src.at[pl.ds(start, rc)],
                dst_ref=dst.at[src_split, pl.ds(dest, rc)],
                send_sem=ss.at[chunk],
                recv_sem=rs.at[src_split, mine],
                device_id={"split": xo},
                device_id_type=MESH,
            )
            for src, dst, ss, rs in pairs[:count]
        ]

    def g_copy(k, o):
        piece = lowx.at[blk, pl.ds(pl.multiple_of(o * rc, rc), rc)]
        return pltpu.make_async_remote_copy(
            src_ref=piece,
            dst_ref=piece,
            send_sem=gsend.at[k - 1, o],
            recv_sem=grecv.at[k - 1, o],
            device_id={"blk": lax.rem(blk + k, nb)},
            device_id_type=MESH,
        )

    def place(i):
        d, j, side = i // (2 * nc), i // 2 % nc, i % 2
        b = jnp.where(side == 0, blk - d, blk + d)
        valid = (b >= 0) & (b < nb) & ((d > 0) | (side == 0))
        return d, j, side, jnp.clip(b, 0, nb - 1), valid

    steps = 2 * nb * nc

    def arrive(i):
        d, j, side, b, valid = place(i)

        @pl.when(valid & (d > 0) & (i < steps))
        def _():
            z_copy(b, j, side).wait_recv()

            @pl.when((side == 0) & (blk < nb - 1))
            def _():
                z_copy(b, j, 0).start()

            @pl.when((side == 1) & (blk > 0))
            def _():
                z_copy(b, j, 1).start()

            for k in range(1, nu):
                c_copy(b, j, k, sub).start()

    def compute(i):
        d, j, side, b, valid = place(i)

        @pl.when(valid & (i >= 0) & (i < steps))
        def _():
            @pl.when(d > 0)
            def _():
                for k in range(1, nu):
                    c_copy(b, j, k, lax.rem(sub - k + nu, nu)).wait_recv()

            start = pl.multiple_of(b * rows + j * rc, rc)
            xo = (b * rows + j * rc) // own
            piece = xall[pl.ds(start, rc), :]
            low = lax.dot_general(
                piece, dnp[...], (((1,), (1,)), ((), ())), preferred_element_type=jnp.float32
            )
            part = jnp.dot(piece, wv[...], preferred_element_type=jnp.float32)

            @pl.when(xo == split)
            def _():
                at = pl.ds(pl.multiple_of(b * rows + j * rc - xo * own, rc), rc)
                lacc[at, :] = low
                acc[at, :] = part

            @pl.when(xo != split)
            def _():
                ls[pl.ds(start, rc), :] = low
                xs[pl.ds(start, rc), :] = part.astype(xs.dtype)
                for copy in x_pair(xo, b, j, split):
                    copy.start()

    def settle(i):
        d, j, side, b, valid = place(i)
        xo = (b * rows + j * rc) // own

        @pl.when(valid & (i >= 0) & (i < steps) & (xo == split))
        def _():
            o = (b * rows + j * rc - xo * own) // rc
            at = pl.ds(pl.multiple_of(o * rc, rc), rc)
            start = pl.multiple_of(b * rows + j * rc, rc)
            low = lacc[at, :]
            for k in range(1, ns):
                src = lax.rem(split + k, ns)
                x_pair(xo, b, j, src, 1)[0].wait_recv()
                low = low + lr[src, at, :]
            lowx[blk, at, :] = (low * mtab[pl.ds(start, rc), :]).astype(lowx.dtype)
            for k in range(1, nb):
                g_copy(k, o).start()

    @pl.loop(0, steps + 4)
    def _(i):
        arrive(i)
        compute(i - 2)
        settle(i - 4)

    for k in range(1, ns):
        for e in range(up_banks):
            u_copy(k, e, lax.rem(split - k + ns, ns)).wait_recv()

    @pl.loop(0, own // rc)
    def _(o):
        at = pl.ds(pl.multiple_of(o * rc, rc), rc)
        value = rv[at, :].astype(jnp.float32) + acc[at, :]
        for k in range(1, ns):
            src = lax.rem(split + k, ns)
            pltpu.make_async_remote_copy(
                src_ref=xs.at[at],
                dst_ref=xr.at[src, at],
                send_sem=xsend.at[o],
                recv_sem=xrecv.at[src, o],
                device_id={"split": src},
                device_id_type=MESH,
            ).wait_recv()
            value = value + xr[src, at, :].astype(jnp.float32)
        for k in range(1, nb):
            g_copy(k, o).wait_recv()
        for p in range(nb):
            value = value + jnp.dot(lowx[p, at, :], upp[p], preferred_element_type=jnp.float32)
        o_ref[at, :] = value.astype(o_ref.dtype)

    for k in range(1, ns):
        for e in range(up_banks):
            u_copy(k, e, split).wait_send()

    @pl.loop(0, own // rc)
    def _(o):
        for k in range(1, nb):
            g_copy(k, o).wait_send()

    @pl.loop(0, nb * nc)
    def _(n):
        b, j = n // nc, n % nc
        xo = (b * rows + j * rc) // own

        @pl.when(xo != split)
        def _():
            for copy in x_pair(xo, b, j, split):
                copy.wait_send()

        @pl.when((b <= blk) & (blk < nb - 1))
        def _():
            z_copy(b, j, 0).wait_send()

        @pl.when((b >= blk) & (blk > 0))
        def _():
            z_copy(b, j, 1).wait_send()

        @pl.when(b != blk)
        def _():
            for k in range(1, nu):
                c_copy(b, j, k, sub).wait_send()


def shards(
    nb, ns, nu,
    attention_output_rows,
    residual,
    output_projection_weight,
    down_adapter_bank,
    up_adapter_bank,
    rollout_row_tenant,
    tenant_bank_entry,
    tenant_live_rank,
):
    rows, feats = attention_output_rows.shape
    own, cols = residual.shape
    banks, rank, _ = down_adapter_bank.shape
    up_banks = up_adapter_bank.shape[0]
    total = rollout_row_tenant.shape[0]
    wide = -(-banks * rank // 128) * 128
    rc = CHUNK_ROWS
    chunks = total // rc
    dma = pltpu.SemaphoreType.DMA
    bf16, f32 = jnp.bfloat16, jnp.float32
    any_spec = pl.BlockSpec(memory_space=pl.ANY)
    smem = pl.BlockSpec(memory_space=pltpu.SMEM)
    vmem = pl.BlockSpec(memory_space=pltpu.VMEM)
    return pl.pallas_call(
        functools.partial(kernel, nb, ns, nu, rc),
        out_shape=jax.ShapeDtypeStruct((own, cols), bf16),
        in_specs=[smem, smem] + [any_spec] * 5 + [vmem],
        out_specs=vmem,
        scratch_shapes=[
            pltpu.VMEM((total, feats), bf16),
            pltpu.VMEM((feats, cols), bf16),
            pltpu.VMEM((own, cols), bf16),
            pltpu.VMEM((wide, feats), bf16),
            pltpu.VMEM((nb, wide, cols), bf16),
            pltpu.VMEM((total, wide), f32),
            pltpu.VMEM((own, cols), f32),
            pltpu.VMEM((own, wide), f32),
            pltpu.VMEM((total, cols), bf16),
            pltpu.VMEM((total, wide), f32),
            pltpu.VMEM((ns, own, cols), bf16),
            pltpu.VMEM((ns, own, wide), f32),
            pltpu.VMEM((nb, own, wide), bf16),
            dma((2 + banks + up_banks,)),
            dma,
            dma((2, chunks)),
            dma((chunks,)),
            dma((nu - 1, chunks)),
            dma((nu - 1, chunks)),
            dma((ns - 1, up_banks)),
            dma((ns - 1, up_banks)),
            dma((chunks,)),
            dma((ns, own // rc)),
            dma((chunks,)),
            dma((ns, own // rc)),
            dma((nb - 1, own // rc)),
            dma((nb - 1, own // rc)),
        ],
        compiler_params=pltpu.CompilerParams(
            collective_id=0, has_side_effects=True, vmem_limit_bytes=48 * 1024 * 1024
        ),
    )(
        tenant_bank_entry,
        tenant_live_rank,
        attention_output_rows,
        residual,
        output_projection_weight,
        down_adapter_bank,
        up_adapter_bank,
        rollout_row_tenant.reshape(1, total),
    )


def solution(mesh):
    in_specs = (
        P(("groups", "blk"), "split"),
        P(("groups", "split"), ("blk", "sub")),
        P("split", ("blk", "sub")),
        P("blk", None, "split"),
        P("split", None, ("blk", "sub")),
        P("groups"),
        P(),
        P(),
    )
    out_specs = P(("groups", "split"), ("blk", "sub"))
    body = functools.partial(
        shards, mesh.shape["blk"], mesh.shape["split"], mesh.shape["sub"]
    )
    return jax.shard_map(body, mesh=mesh, in_specs=in_specs, out_specs=out_specs, check_vma=False)
```

```python
import functools

import jax
import jax.numpy as jnp
from jax import lax
from jax.experimental import pallas as pl
from jax.experimental.pallas import tpu as pltpu
from jax.sharding import PartitionSpec as P

CHUNK_ROWS = 64
MESH = pl.DeviceIdType.MESH


def kernel(
    nb, ns, nu, rc,
    ent_ref, rank_ref, x_ref, r_ref, w_ref, dn_ref, up_ref, ten_ref, o_ref,
    xall, wv, rv, dnp, upp, mtab, acc, lacc, xs, ls, xr, lr, lowx,
    sem_loc, sem_own, zsend, zrecv, csend, crecv, usend, urecv,
    xsend, xrecv, lsend, lrecv, gsend, grecv,
):
    blk, split, sub = lax.axis_index("blk"), lax.axis_index("split"), lax.axis_index("sub")
    rows, feats = x_ref.shape
    cols = w_ref.shape[1]
    own = r_ref.shape[0]
    banks, rank = dn_ref.shape[0], dn_ref.shape[1]
    up_banks = up_ref.shape[0]
    wide = dnp.shape[0]
    total = ten_ref.shape[1]
    tenants = ent_ref.shape[0]
    nc = rows // rc
    half = rc // nu

    w_copy = pltpu.make_async_copy(w_ref, wv, sem_loc.at[0])
    w_copy.start()
    x_copy = pltpu.make_async_copy(
        x_ref, xall.at[pl.ds(pl.multiple_of(blk * rows, rows), rows)], sem_own
    )
    x_copy.start()
    loads = [pltpu.make_async_copy(r_ref, rv, sem_loc.at[1])]
    for e in range(banks):
        loads.append(
            pltpu.make_async_copy(dn_ref.at[e], dnp.at[pl.ds(e * rank, rank)], sem_loc.at[2 + e])
        )

    def up_slot(bank):
        return upp.at[bank // banks, pl.ds(pl.multiple_of(bank % banks * rank, rank), rank)]

    for e in range(up_banks):
        loads.append(
            pltpu.make_async_copy(
                up_ref.at[e], up_slot(split * up_banks + e), sem_loc.at[2 + banks + e]
            )
        )
    for load in loads:
        load.start()

    barrier = pltpu.get_barrier_semaphore()
    for k in range(1, nb):
        pl.semaphore_signal(
            barrier, inc=1, device_id={"blk": lax.rem(blk + k, nb)}, device_id_type=MESH
        )
    for k in range(1, ns):
        pl.semaphore_signal(
            barrier, inc=1, device_id={"split": lax.rem(split + k, ns)}, device_id_type=MESH
        )
    for k in range(1, nu):
        pl.semaphore_signal(
            barrier, inc=1, device_id={"sub": lax.rem(sub + k, nu)}, device_id_type=MESH
        )
    pl.semaphore_wait(barrier, nb + ns + nu - 3)

    def half_rows(ref, b, j, core):
        start = pl.multiple_of(b * rows + j * rc + core * half, half)
        return ref.at[pl.ds(start, half)]

    def z_copy(b, j, side, src=None):
        dst = half_rows(xall, b, j, sub)
        return pltpu.make_async_remote_copy(
            src_ref=dst if src is None else src,
            dst_ref=dst,
            send_sem=zsend.at[side, b * nc + j],
            recv_sem=zrecv.at[b * nc + j],
            device_id={"blk": lax.rem(blk + 1 - 2 * side + nb, nb)},
            device_id_type=MESH,
        )

    def c_copy(b, j, k, core):
        piece = half_rows(xall, b, j, core)
        return pltpu.make_async_remote_copy(
            src_ref=piece,
            dst_ref=piece,
            send_sem=csend.at[k - 1, b * nc + j],
            recv_sem=crecv.at[k - 1, b * nc + j],
            device_id={"sub": lax.rem(sub + k, nu)},
            device_id_type=MESH,
        )

    for j in range(nc):
        src = x_ref.at[pl.ds(pl.multiple_of(j * rc + sub * half, half), half)]

        @pl.when(blk < nb - 1)
        def _():
            z_copy(blk, j, 0, src).start()

        @pl.when(blk > 0)
        def _():
            z_copy(blk, j, 1, src).start()

    def u_copy(k, e, owner):
        return pltpu.make_async_remote_copy(
            src_ref=up_ref.at[e],
            dst_ref=up_slot(owner * up_banks + e),
            send_sem=usend.at[k - 1, e],
            recv_sem=urecv.at[k - 1, e],
            device_id={"split": lax.rem(split + k, ns)},
            device_id_type=MESH,
        )

    for k in range(1, ns):
        for e in range(up_banks):
            u_copy(k, e, split).start()

    if wide > banks * rank:
        pad = wide - banks * rank
        dnp[pl.ds(banks * rank, pad), :] = jnp.zeros((pad, feats), dnp.dtype)
        for p in range(nb):
            upp[p, pl.ds(banks * rank, pad), :] = jnp.zeros((pad, cols), upp.dtype)
    lane = lax.broadcasted_iota(jnp.int32, (1, wide), 1)
    tcol = jnp.transpose(
        jnp.broadcast_to(ten_ref[...].astype(jnp.float32), (8, total))
    )[:, :1]
    table = jnp.zeros((total, wide), jnp.float32)
    for t in range(tenants):
        live = jnp.full((1, wide), rank_ref[t], jnp.int32)
        slot = jnp.full((1, wide), ent_ref[t], jnp.int32)
        line = jnp.zeros((1, wide), jnp.float32)
        for e in range(banks):
            keep = (
                (lane >= e * rank) & (lane < e * rank + jnp.minimum(live, rank))
                & (slot == blk * banks + e)
            )
            line = jnp.where(keep, rank / live.astype(jnp.float32), line)
        table = jnp.where(tcol == t, line, table)
    mtab[...] = table

    for load in loads:
        load.wait()
    x_copy.wait()
    w_copy.wait()

    def x_pair(xo, b, j, src_split, count=2):
        start = pl.multiple_of(b * rows + j * rc, rc)
        dest = pl.multiple_of(b * rows + j * rc - xo * own, rc)
        chunk, mine = b * nc + j, (b * rows + j * rc - xo * own) // rc
        pairs = ((ls, lr, lsend, lrecv), (xs, xr, xsend, xrecv))
        return [
            pltpu.make_async_remote_copy(
                src_ref=src.at[pl.ds(start, rc)],
                dst_ref=dst.at[src_split, pl.ds(dest, rc)],
                send_sem=ss.at[chunk],
                recv_sem=rs.at[src_split, mine],
                device_id={"split": xo},
                device_id_type=MESH,
            )
            for src, dst, ss, rs in pairs[:count]
        ]

    def g_copy(k, o):
        piece = lowx.at[blk, pl.ds(pl.multiple_of(o * rc, rc), rc)]
        return pltpu.make_async_remote_copy(
            src_ref=piece,
            dst_ref=piece,
            send_sem=gsend.at[k - 1, o],
            recv_sem=grecv.at[k - 1, o],
            device_id={"blk": lax.rem(blk + k, nb)},
            device_id_type=MESH,
        )

    def place(i):
        d, j, side = i // (2 * nc), i // 2 % nc, i % 2
        b = jnp.where(side == 0, blk - d, blk + d)
        valid = (b >= 0) & (b < nb) & ((d > 0) | (side == 0))
        return d, j, side, jnp.clip(b, 0, nb - 1), valid

    steps = 2 * nb * nc

    def arrive(i):
        d, j, side, b, valid = place(i)

        @pl.when(valid & (d > 0) & (i < steps))
        def _():
            z_copy(b, j, side).wait_recv()

            @pl.when((side == 0) & (blk < nb - 1))
            def _():
                z_copy(b, j, 0).start()

            @pl.when((side == 1) & (blk > 0))
            def _():
                z_copy(b, j, 1).start()

            for k in range(1, nu):
                c_copy(b, j, k, sub).start()

    def compute(i):
        d, j, side, b, valid = place(i)

        @pl.when(valid & (i >= 0) & (i < steps))
        def _():
            @pl.when(d > 0)
            def _():
                for k in range(1, nu):
                    c_copy(b, j, k, lax.rem(sub - k + nu, nu)).wait_recv()

            start = pl.multiple_of(b * rows + j * rc, rc)
            xo = (b * rows + j * rc) // own
            piece = xall[pl.ds(start, rc), :]
            low = lax.dot_general(
                piece, dnp[...], (((1,), (1,)), ((), ())), preferred_element_type=jnp.float32
            )
            part = jnp.dot(piece, wv[...], preferred_element_type=jnp.float32)

            @pl.when(xo == split)
            def _():
                at = pl.ds(pl.multiple_of(b * rows + j * rc - xo * own, rc), rc)
                lacc[at, :] = low
                acc[at, :] = part

            @pl.when(xo != split)
            def _():
                ls[pl.ds(start, rc), :] = low
                xs[pl.ds(start, rc), :] = part.astype(xs.dtype)
                for copy in x_pair(xo, b, j, split):
                    copy.start()

    def settle(i):
        d, j, side, b, valid = place(i)
        xo = (b * rows + j * rc) // own

        @pl.when(valid & (i >= 0) & (i < steps) & (xo == split))
        def _():
            o = (b * rows + j * rc - xo * own) // rc
            at = pl.ds(pl.multiple_of(o * rc, rc), rc)
            start = pl.multiple_of(b * rows + j * rc, rc)
            low = lacc[at, :]
            for k in range(1, ns):
                src = lax.rem(split + k, ns)
                x_pair(xo, b, j, src, 1)[0].wait_recv()
                low = low + lr[src, at, :]
            lowx[blk, at, :] = (low * mtab[pl.ds(start, rc), :]).astype(lowx.dtype)
            for k in range(1, nb):
                g_copy(k, o).start()

    @pl.loop(0, steps + 4)
    def _(i):
        arrive(i)
        compute(i - 2)
        settle(i - 4)

    for k in range(1, ns):
        for e in range(up_banks):
            u_copy(k, e, lax.rem(split - k + ns, ns)).wait_recv()

    @pl.loop(0, own // rc)
    def _(o):
        at = pl.ds(pl.multiple_of(o * rc, rc), rc)
        value = rv[at, :].astype(jnp.float32) + acc[at, :]
        for k in range(1, ns):
            src = lax.rem(split + k, ns)
            pltpu.make_async_remote_copy(
                src_ref=xs.at[at],
                dst_ref=xr.at[src, at],
                send_sem=xsend.at[o],
                recv_sem=xrecv.at[src, o],
                device_id={"split": src},
                device_id_type=MESH,
            ).wait_recv()
            value = value + xr[src, at, :].astype(jnp.float32)
        for k in range(1, nb):
            g_copy(k, o).wait_recv()
        for p in range(nb):
            value = value + jnp.dot(lowx[p, at, :], upp[p], preferred_element_type=jnp.float32)
        o_ref[at, :] = value.astype(o_ref.dtype)

    for k in range(1, ns):
        for e in range(up_banks):
            u_copy(k, e, split).wait_send()

    @pl.loop(0, own // rc)
    def _(o):
        for k in range(1, nb):
            g_copy(k, o).wait_send()

    @pl.loop(0, nb * nc)
    def _(n):
        b, j = n // nc, n % nc
        xo = (b * rows + j * rc) // own

        @pl.when(xo != split)
        def _():
            for copy in x_pair(xo, b, j, split):
                copy.wait_send()

        @pl.when((b <= blk) & (blk < nb - 1))
        def _():
            z_copy(b, j, 0).wait_send()

        @pl.when((b >= blk) & (blk > 0))
        def _():
            z_copy(b, j, 1).wait_send()

        @pl.when(b != blk)
        def _():
            for k in range(1, nu):
                c_copy(b, j, k, sub).wait_send()


def shards(
    nb, ns, nu,
    attention_output_rows,
    residual,
    output_projection_weight,
    down_adapter_bank,
    up_adapter_bank,
    rollout_row_tenant,
    tenant_bank_entry,
    tenant_live_rank,
):
    rows, feats = attention_output_rows.shape
    own, cols = residual.shape
    banks, rank, _ = down_adapter_bank.shape
    up_banks = up_adapter_bank.shape[0]
    total = rollout_row_tenant.shape[0]
    wide = -(-banks * rank // 128) * 128
    rc = CHUNK_ROWS
    chunks = total // rc
    dma = pltpu.SemaphoreType.DMA
    bf16, f32 = jnp.bfloat16, jnp.float32
    any_spec = pl.BlockSpec(memory_space=pl.ANY)
    smem = pl.BlockSpec(memory_space=pltpu.SMEM)
    vmem = pl.BlockSpec(memory_space=pltpu.VMEM)
    return pl.pallas_call(
        functools.partial(kernel, nb, ns, nu, rc),
        out_shape=jax.ShapeDtypeStruct((own, cols), bf16),
        in_specs=[smem, smem] + [any_spec] * 5 + [vmem],
        out_specs=vmem,
        scratch_shapes=[
            pltpu.VMEM((total, feats), bf16),
            pltpu.VMEM((feats, cols), bf16),
            pltpu.VMEM((own, cols), bf16),
            pltpu.VMEM((wide, feats), bf16),
            pltpu.VMEM((nb, wide, cols), bf16),
            pltpu.VMEM((total, wide), f32),
            pltpu.VMEM((own, cols), f32),
            pltpu.VMEM((own, wide), f32),
            pltpu.VMEM((total, cols), bf16),
            pltpu.VMEM((total, wide), f32),
            pltpu.VMEM((ns, own, cols), bf16),
            pltpu.VMEM((ns, own, wide), f32),
            pltpu.VMEM((nb, own, wide), bf16),
            dma((2 + banks + up_banks,)),
            dma,
            dma((2, chunks)),
            dma((chunks,)),
            dma((nu - 1, chunks)),
            dma((nu - 1, chunks)),
            dma((ns - 1, up_banks)),
            dma((ns - 1, up_banks)),
            dma((chunks,)),
            dma((ns, own // rc)),
            dma((chunks,)),
            dma((ns, own // rc)),
            dma((nb - 1, own // rc)),
            dma((nb - 1, own // rc)),
        ],
        compiler_params=pltpu.CompilerParams(
            collective_id=0, has_side_effects=True
        ),
    )(
        tenant_bank_entry,
        tenant_live_rank,
        attention_output_rows,
        residual,
        output_projection_weight,
        down_adapter_bank,
        up_adapter_bank,
        rollout_row_tenant.reshape(1, total),
    )


def solution(mesh):
    in_specs = (
        P(("groups", "blk"), "split"),
        P(("groups", "split"), ("blk", "sub")),
        P("split", ("blk", "sub")),
        P("blk", None, "split"),
        P("split", None, ("blk", "sub")),
        P("groups"),
        P(),
        P(),
    )
    out_specs = P(("groups", "split"), ("blk", "sub"))
    body = functools.partial(
        shards, mesh.shape["blk"], mesh.shape["split"], mesh.shape["sub"]
    )
    return jax.shard_map(body, mesh=mesh, in_specs=in_specs, out_specs=out_specs, check_vma=False)
```

```python
import functools

import jax
import jax.numpy as jnp
from jax import lax
from jax.experimental import pallas as pl
from jax.experimental.pallas import tpu as pltpu
from jax.sharding import PartitionSpec as P

CHUNK_ROWS = 64
MESH = pl.DeviceIdType.MESH


def kernel(
    nb, ns, nu, rc,
    ent_ref, rank_ref, x_ref, r_ref, w_ref, dn_ref, up_ref, ten_ref, o_ref,
    xall, wv, rv, dnp, upp, mtab, acc, lacc, xs, ls, xr, lr, lowx,
    sem_loc, sem_own, zsend, zrecv, csend, crecv, usend, urecv,
    xsend, xrecv, lsend, lrecv, gsend, grecv, fsend, frecv, bsend, brecv,
):
    blk, split, sub = lax.axis_index("blk"), lax.axis_index("split"), lax.axis_index("sub")
    rows, feats = x_ref.shape
    cols = w_ref.shape[1]
    own = r_ref.shape[0]
    banks, rank = dn_ref.shape[0], dn_ref.shape[1]
    up_banks = up_ref.shape[0]
    wide = dnp.shape[0]
    total = ten_ref.shape[1]
    tenants = ent_ref.shape[0]
    nc = rows // rc
    half = rc // nu
    group = nb // 2
    upper = blk // group
    middle = group - 1 + upper
    in_middle = blk == middle
    share = own // nu

    w_copy = pltpu.make_async_copy(w_ref, wv, sem_loc.at[0])
    w_copy.start()
    x_copy = pltpu.make_async_copy(
        x_ref, xall.at[pl.ds(pl.multiple_of(blk * rows, rows), rows)], sem_own
    )
    x_copy.start()
    loads = [pltpu.make_async_copy(r_ref, rv, sem_loc.at[1])]

    def bank_slot(place, e):
        return dnp.at[pl.ds(pl.multiple_of((place * banks + e) * rank, rank), rank)]

    bank_loads = [
        pltpu.make_async_copy(dn_ref.at[e], bank_slot(blk % group, e), sem_loc.at[2 + e])
        for e in range(banks)
    ]

    def up_slot(bank):
        return upp.at[pl.ds(pl.multiple_of(bank * rank, rank), rank)]

    for e in range(up_banks):
        loads.append(
            pltpu.make_async_copy(
                up_ref.at[e], up_slot(split * up_banks + e), sem_loc.at[2 + banks + e]
            )
        )
    for load in loads:
        load.start()

    @pl.when(in_middle)
    def _():
        for load in bank_loads:
            load.start()

    barrier = pltpu.get_barrier_semaphore()
    for k in range(1, nb):
        pl.semaphore_signal(
            barrier, inc=1, device_id={"blk": lax.rem(blk + k, nb)}, device_id_type=MESH
        )
    for k in range(1, ns):
        pl.semaphore_signal(
            barrier, inc=1, device_id={"split": lax.rem(split + k, ns)}, device_id_type=MESH
        )
    for k in range(1, nu):
        pl.semaphore_signal(
            barrier, inc=1, device_id={"sub": lax.rem(sub + k, nu)}, device_id_type=MESH
        )
    pl.semaphore_wait(barrier, nb + ns + nu - 3)

    def half_rows(ref, b, j, core):
        start = pl.multiple_of(b * rows + j * rc + core * half, half)
        return ref.at[pl.ds(start, half)]

    def z_copy(b, j, side, src=None):
        dst = half_rows(xall, b, j, sub)
        return pltpu.make_async_remote_copy(
            src_ref=dst if src is None else src,
            dst_ref=dst,
            send_sem=zsend.at[side, b * nc + j],
            recv_sem=zrecv.at[b * nc + j],
            device_id={"blk": lax.rem(blk + 1 - 2 * side + nb, nb)},
            device_id_type=MESH,
        )

    def c_copy(b, j, k, core):
        piece = half_rows(xall, b, j, core)
        return pltpu.make_async_remote_copy(
            src_ref=piece,
            dst_ref=piece,
            send_sem=csend.at[k - 1, b * nc + j],
            recv_sem=crecv.at[k - 1, b * nc + j],
            device_id={"sub": lax.rem(sub + k, nu)},
            device_id_type=MESH,
        )

    for j in range(nc):
        src = x_ref.at[pl.ds(pl.multiple_of(j * rc + sub * half, half), half)]

        @pl.when(blk < nb - 1)
        def _():
            z_copy(blk, j, 0, src).start()

        @pl.when(blk > 0)
        def _():
            z_copy(blk, j, 1, src).start()

    def b_copy(e, place):
        return pltpu.make_async_remote_copy(
            src_ref=dn_ref.at[e],
            dst_ref=bank_slot(place, e),
            send_sem=bsend.at[e],
            recv_sem=brecv.at[place, e],
            device_id={"blk": middle},
            device_id_type=MESH,
        )

    @pl.when(jnp.logical_not(in_middle))
    def _():
        for e in range(banks):
            b_copy(e, blk % group).start()

    def u_copy(k, e, owner):
        return pltpu.make_async_remote_copy(
            src_ref=up_ref.at[e],
            dst_ref=up_slot(owner * up_banks + e),
            send_sem=usend.at[k - 1, e],
            recv_sem=urecv.at[k - 1, e],
            device_id={"split": lax.rem(split + k, ns)},
            device_id_type=MESH,
        )

    for k in range(1, ns):
        for e in range(up_banks):
            u_copy(k, e, split).start()

    lane = lax.broadcasted_iota(jnp.int32, (1, wide), 1)
    tcol = jnp.transpose(
        jnp.broadcast_to(ten_ref[...].astype(jnp.float32), (8, total))
    )[:, :1]
    table = jnp.zeros((total, wide), jnp.float32)
    for t in range(tenants):
        live = jnp.full((1, wide), rank_ref[t], jnp.int32)
        slot = jnp.full((1, wide), ent_ref[t], jnp.int32)
        line = jnp.zeros((1, wide), jnp.float32)
        for e in range(group * banks):
            keep = (
                (lane >= e * rank) & (lane < e * rank + jnp.minimum(live, rank))
                & (slot == upper * group * banks + e)
            )
            line = jnp.where(keep, rank / live.astype(jnp.float32), line)
        table = jnp.where(tcol == t, line, table)
    mtab[...] = table

    for load in loads:
        load.wait()
    x_copy.wait()
    w_copy.wait()

    def x_copy_of(src, dst, ss, rs, xo, b, j, src_split):
        start = pl.multiple_of(b * rows + j * rc, rc)
        dest = pl.multiple_of(b * rows + j * rc - xo * own, rc)
        return pltpu.make_async_remote_copy(
            src_ref=src.at[pl.ds(start, rc)],
            dst_ref=dst.at[src_split, pl.ds(dest, rc)],
            send_sem=ss.at[b * nc + j],
            recv_sem=rs.at[src_split, dest // rc],
            device_id={"split": xo},
            device_id_type=MESH,
        )

    def p_copy(*where):
        return x_copy_of(xs, xr, xsend, xrecv, *where)

    def l_copy(*where):
        return x_copy_of(ls, lr, lsend, lrecv, *where)

    def share_of(h, core):
        return lowx.at[h, pl.ds(pl.multiple_of(core * share, share), share)]

    def g_copy(k, h):
        return pltpu.make_async_remote_copy(
            src_ref=share_of(h, sub),
            dst_ref=share_of(h, sub),
            send_sem=gsend.at[k - 1],
            recv_sem=grecv.at[h],
            device_id={"blk": lax.rem(blk + k, nb)},
            device_id_type=MESH,
        )

    def f_copy(k, h, core):
        return pltpu.make_async_remote_copy(
            src_ref=share_of(h, core),
            dst_ref=share_of(h, core),
            send_sem=fsend.at[k - 1, h],
            recv_sem=frecv.at[k - 1, h],
            device_id={"sub": lax.rem(sub + k, nu)},
            device_id_type=MESH,
        )

    def place(i):
        d, j, side = i // (2 * nc), i // 2 % nc, i % 2
        b = jnp.where(side == 0, blk - d, blk + d)
        valid = (b >= 0) & (b < nb) & ((d > 0) | (side == 0))
        return d, j, side, jnp.clip(b, 0, nb - 1), valid

    steps = 2 * nb * nc

    def arrive(i):
        d, j, side, b, valid = place(i)

        @pl.when(valid & (d > 0) & (i < steps))
        def _():
            z_copy(b, j, side).wait_recv()

            @pl.when((side == 0) & (blk < nb - 1))
            def _():
                z_copy(b, j, 0).start()

            @pl.when((side == 1) & (blk > 0))
            def _():
                z_copy(b, j, 1).start()

            for k in range(1, nu):
                c_copy(b, j, k, sub).start()

    def compute(i):
        d, j, side, b, valid = place(i)

        @pl.when(valid & (i >= 0) & (i < steps))
        def _():
            @pl.when(d > 0)
            def _():
                for k in range(1, nu):
                    c_copy(b, j, k, lax.rem(sub - k + nu, nu)).wait_recv()

            start = pl.multiple_of(b * rows + j * rc, rc)
            xo = (b * rows + j * rc) // own
            piece = xall[pl.ds(start, rc), :]
            part = jnp.dot(piece, wv[...], preferred_element_type=jnp.float32)

            @pl.when(xo == split)
            def _():
                at = pl.ds(pl.multiple_of(b * rows + j * rc - xo * own, rc), rc)
                acc[at, :] = part

            @pl.when(xo != split)
            def _():
                xs[pl.ds(start, rc), :] = part.astype(xs.dtype)
                p_copy(xo, b, j, split).start()

    @pl.loop(0, steps + 2)
    def _(i):
        arrive(i)
        compute(i - 2)

    @pl.when(in_middle)
    def _():
        for load in bank_loads:
            load.wait()
        for p in range(group):
            @pl.when(p != blk % group)
            def _():
                for e in range(banks):
                    b_copy(e, p).wait_recv()

        @pl.loop(0, nb * nc)
        def _(n):
            b, j = n // nc, n % nc
            start = pl.multiple_of(n * rc, rc)
            xo = (n * rc) // own
            low = lax.dot_general(
                xall[pl.ds(start, rc), :], dnp[...], (((1,), (1,)), ((), ())),
                preferred_element_type=jnp.float32,
            )

            @pl.when(xo == split)
            def _():
                lacc[pl.ds(pl.multiple_of(n * rc - xo * own, rc), rc), :] = low

            @pl.when(xo != split)
            def _():
                ls[pl.ds(start, rc), :] = low
                l_copy(xo, b, j, split).start()

        @pl.loop(0, own // rc)
        def _(o):
            at = pl.ds(pl.multiple_of(o * rc, rc), rc)
            n = split * (own // rc) + o
            low = lacc[at, :]
            for k in range(1, ns):
                src = lax.rem(split + k, ns)
                l_copy(split, n // nc, n % nc, src).wait_recv()
                low = low + lr[src, at, :]
            scale = mtab[pl.ds(pl.multiple_of(n * rc, rc), rc), :]
            lowx[upper, at, :] = (low * scale).astype(lowx.dtype)

        for k in range(1, nb):
            g_copy(k, upper).start()

    def from_far(h):
        return jnp.logical_not(in_middle & (upper == h))

    for h in range(2):
        @pl.when(from_far(h))
        def _():
            g_copy(1, h).wait_recv()
            for k in range(1, nu):
                f_copy(k, h, sub).start()
    for h in range(2):
        @pl.when(from_far(h))
        def _():
            for k in range(1, nu):
                f_copy(k, h, lax.rem(sub - k + nu, nu)).wait_recv()

    for k in range(1, ns):
        for e in range(up_banks):
            u_copy(k, e, lax.rem(split - k + ns, ns)).wait_recv()

    @pl.loop(0, own // rc)
    def _(o):
        at = pl.ds(pl.multiple_of(o * rc, rc), rc)
        value = rv[at, :].astype(jnp.float32) + acc[at, :]
        for k in range(1, ns):
            src = lax.rem(split + k, ns)
            pltpu.make_async_remote_copy(
                src_ref=xs.at[at],
                dst_ref=xr.at[src, at],
                send_sem=xsend.at[o],
                recv_sem=xrecv.at[src, o],
                device_id={"split": src},
                device_id_type=MESH,
            ).wait_recv()
            value = value + xr[src, at, :].astype(jnp.float32)
        for h in range(2):
            value = value + jnp.dot(
                lowx[h, at, :], upp[h * wide:(h + 1) * wide, :],
                preferred_element_type=jnp.float32,
            )
        o_ref[at, :] = value.astype(o_ref.dtype)

    for k in range(1, ns):
        for e in range(up_banks):
            u_copy(k, e, split).wait_send()

    @pl.when(in_middle)
    def _():
        for k in range(1, nb):
            g_copy(k, upper).wait_send()

    @pl.when(jnp.logical_not(in_middle))
    def _():
        for e in range(banks):
            b_copy(e, blk % group).wait_send()

    for h in range(2):
        @pl.when(from_far(h))
        def _():
            for k in range(1, nu):
                f_copy(k, h, sub).wait_send()

    @pl.loop(0, nb * nc)
    def _(n):
        b, j = n // nc, n % nc
        xo = (b * rows + j * rc) // own

        @pl.when(xo != split)
        def _():
            p_copy(xo, b, j, split).wait_send()

            @pl.when(in_middle)
            def _():
                l_copy(xo, b, j, split).wait_send()

        @pl.when((b <= blk) & (blk < nb - 1))
        def _():
            z_copy(b, j, 0).wait_send()

        @pl.when((b >= blk) & (blk > 0))
        def _():
            z_copy(b, j, 1).wait_send()

        @pl.when(b != blk)
        def _():
            for k in range(1, nu):
                c_copy(b, j, k, sub).wait_send()


def shards(
    nb, ns, nu,
    attention_output_rows,
    residual,
    output_projection_weight,
    down_adapter_bank,
    up_adapter_bank,
    rollout_row_tenant,
    tenant_bank_entry,
    tenant_live_rank,
):
    rows, feats = attention_output_rows.shape
    own, cols = residual.shape
    banks, rank, _ = down_adapter_bank.shape
    up_banks = up_adapter_bank.shape[0]
    total = rollout_row_tenant.shape[0]
    wide = nb // 2 * banks * rank
    rc = CHUNK_ROWS
    chunks = total // rc
    dma = pltpu.SemaphoreType.DMA
    bf16, f32 = jnp.bfloat16, jnp.float32
    any_spec = pl.BlockSpec(memory_space=pl.ANY)
    smem = pl.BlockSpec(memory_space=pltpu.SMEM)
    vmem = pl.BlockSpec(memory_space=pltpu.VMEM)
    return pl.pallas_call(
        functools.partial(kernel, nb, ns, nu, rc),
        out_shape=jax.ShapeDtypeStruct((own, cols), bf16),
        in_specs=[smem, smem] + [any_spec] * 5 + [vmem],
        out_specs=vmem,
        scratch_shapes=[
            pltpu.VMEM((total, feats), bf16),
            pltpu.VMEM((feats, cols), bf16),
            pltpu.VMEM((own, cols), bf16),
            pltpu.VMEM((wide, feats), bf16),
            pltpu.VMEM((2 * wide, cols), bf16),
            pltpu.VMEM((total, wide), f32),
            pltpu.VMEM((own, cols), f32),
            pltpu.VMEM((own, wide), f32),
            pltpu.VMEM((total, cols), bf16),
            pltpu.VMEM((total, wide), f32),
            pltpu.VMEM((ns, own, cols), bf16),
            pltpu.VMEM((ns, own, wide), f32),
            pltpu.VMEM((2, own, wide), bf16),
            dma((2 + banks + up_banks,)),
            dma,
            dma((2, chunks)),
            dma((chunks,)),
            dma((nu - 1, chunks)),
            dma((nu - 1, chunks)),
            dma((ns - 1, up_banks)),
            dma((ns - 1, up_banks)),
            dma((chunks,)),
            dma((ns, own // rc)),
            dma((chunks,)),
            dma((ns, own // rc)),
            dma((nb - 1,)),
            dma((2,)),
            dma((nu - 1, 2)),
            dma((nu - 1, 2)),
            dma((banks,)),
            dma((nb // 2, banks)),
        ],
        compiler_params=pltpu.CompilerParams(
            collective_id=0, has_side_effects=True
        ),
    )(
        tenant_bank_entry,
        tenant_live_rank,
        attention_output_rows,
        residual,
        output_projection_weight,
        down_adapter_bank,
        up_adapter_bank,
        rollout_row_tenant.reshape(1, total),
    )


def solution(mesh):
    in_specs = (
        P(("groups", "blk"), "split"),
        P(("groups", "split"), ("blk", "sub")),
        P("split", ("blk", "sub")),
        P("blk", None, "split"),
        P("split", None, ("blk", "sub")),
        P("groups"),
        P(),
        P(),
    )
    out_specs = P(("groups", "split"), ("blk", "sub"))
    body = functools.partial(
        shards, mesh.shape["blk"], mesh.shape["split"], mesh.shape["sub"]
    )
    return jax.shard_map(body, mesh=mesh, in_specs=in_specs, out_specs=out_specs, check_vma=False)
```

```python
import functools

import jax
import jax.numpy as jnp
from jax import lax
from jax.experimental import pallas as pl
from jax.experimental.pallas import tpu as pltpu
from jax.sharding import PartitionSpec as P

CHUNK_ROWS = 64
PARTS = 2
MESH = pl.DeviceIdType.MESH


def kernel(
    nb, ns, nu, rc,
    ent_ref, rank_ref, x_ref, r_ref, w_ref, dn_ref, up_ref, ten_ref, o_ref,
    xall, wv, rv, dnp, upp, mtab, acc, lacc, xs, ls, xr, lr, lowx,
    sem_loc, sem_own, zsend, zrecv, csend, crecv, usend, urecv,
    xsend, xrecv, lsend, lrecv, gsend, grecv, fsend, frecv, bsend, brecv,
):
    blk, split, sub = lax.axis_index("blk"), lax.axis_index("split"), lax.axis_index("sub")
    rows, feats = x_ref.shape
    cols = w_ref.shape[1]
    own = r_ref.shape[0]
    banks, rank = dn_ref.shape[0], dn_ref.shape[1]
    up_banks = up_ref.shape[0]
    wide = dnp.shape[0]
    total = ten_ref.shape[1]
    tenants = ent_ref.shape[0]
    nc = rows // rc
    half = rc // nu
    group = nb // 2
    upper = blk // group
    middle = group - 1 + upper
    in_middle = blk == middle
    share = own // nu

    w_copy = pltpu.make_async_copy(w_ref, wv, sem_loc.at[0])
    w_copy.start()
    x_copy = pltpu.make_async_copy(
        x_ref, xall.at[pl.ds(pl.multiple_of(blk * rows, rows), rows)], sem_own
    )
    x_copy.start()
    loads = [pltpu.make_async_copy(r_ref, rv, sem_loc.at[1])]

    def bank_slot(place, e):
        return dnp.at[pl.ds(pl.multiple_of((place * banks + e) * rank, rank), rank)]

    bank_loads = [
        pltpu.make_async_copy(dn_ref.at[e], bank_slot(blk % group, e), sem_loc.at[2 + e])
        for e in range(banks)
    ]

    def up_slot(bank):
        return upp.at[pl.ds(pl.multiple_of(bank * rank, rank), rank)]

    for e in range(up_banks):
        loads.append(
            pltpu.make_async_copy(
                up_ref.at[e], up_slot(split * up_banks + e), sem_loc.at[2 + banks + e]
            )
        )
    for load in loads:
        load.start()

    @pl.when(in_middle)
    def _():
        for load in bank_loads:
            load.start()

    barrier = pltpu.get_barrier_semaphore()
    for k in range(1, nb):
        pl.semaphore_signal(
            barrier, inc=1, device_id={"blk": lax.rem(blk + k, nb)}, device_id_type=MESH
        )
    for k in range(1, ns):
        pl.semaphore_signal(
            barrier, inc=1, device_id={"split": lax.rem(split + k, ns)}, device_id_type=MESH
        )
    for k in range(1, nu):
        pl.semaphore_signal(
            barrier, inc=1, device_id={"sub": lax.rem(sub + k, nu)}, device_id_type=MESH
        )
    pl.semaphore_wait(barrier, nb + ns + nu - 3)

    def half_rows(ref, b, j, core):
        start = pl.multiple_of(b * rows + j * rc + core * half, half)
        return ref.at[pl.ds(start, half)]

    def z_copy(b, j, side, src=None):
        dst = half_rows(xall, b, j, sub)
        return pltpu.make_async_remote_copy(
            src_ref=dst if src is None else src,
            dst_ref=dst,
            send_sem=zsend.at[side, b * nc + j],
            recv_sem=zrecv.at[b * nc + j],
            device_id={"blk": lax.rem(blk + 1 - 2 * side + nb, nb)},
            device_id_type=MESH,
        )

    def c_copy(b, j, k, core):
        piece = half_rows(xall, b, j, core)
        return pltpu.make_async_remote_copy(
            src_ref=piece,
            dst_ref=piece,
            send_sem=csend.at[k - 1, b * nc + j],
            recv_sem=crecv.at[k - 1, b * nc + j],
            device_id={"sub": lax.rem(sub + k, nu)},
            device_id_type=MESH,
        )

    for j in range(nc):
        src = x_ref.at[pl.ds(pl.multiple_of(j * rc + sub * half, half), half)]

        @pl.when(blk < nb - 1)
        def _():
            z_copy(blk, j, 0, src).start()

        @pl.when(blk > 0)
        def _():
            z_copy(blk, j, 1, src).start()

    def b_copy(e, place):
        return pltpu.make_async_remote_copy(
            src_ref=dn_ref.at[e],
            dst_ref=bank_slot(place, e),
            send_sem=bsend.at[e],
            recv_sem=brecv.at[place, e],
            device_id={"blk": middle},
            device_id_type=MESH,
        )

    @pl.when(jnp.logical_not(in_middle))
    def _():
        for e in range(banks):
            b_copy(e, blk % group).start()

    def u_copy(k, e, owner):
        return pltpu.make_async_remote_copy(
            src_ref=up_ref.at[e],
            dst_ref=up_slot(owner * up_banks + e),
            send_sem=usend.at[k - 1, e],
            recv_sem=urecv.at[k - 1, e],
            device_id={"split": lax.rem(split + k, ns)},
            device_id_type=MESH,
        )

    for k in range(1, ns):
        for e in range(up_banks):
            u_copy(k, e, split).start()

    lane = lax.broadcasted_iota(jnp.int32, (1, wide), 1)
    tcol = jnp.transpose(
        jnp.broadcast_to(ten_ref[...].astype(jnp.float32), (8, total))
    )[:, :1]
    table = jnp.zeros((total, wide), jnp.float32)
    for t in range(tenants):
        live = jnp.full((1, wide), rank_ref[t], jnp.int32)
        slot = jnp.full((1, wide), ent_ref[t], jnp.int32)
        line = jnp.zeros((1, wide), jnp.float32)
        for e in range(group * banks):
            keep = (
                (lane >= e * rank) & (lane < e * rank + jnp.minimum(live, rank))
                & (slot == upper * group * banks + e)
            )
            line = jnp.where(keep, rank / live.astype(jnp.float32), line)
        table = jnp.where(tcol == t, line, table)
    mtab[...] = table

    for load in loads:
        load.wait()
    x_copy.wait()
    w_copy.wait()

    def x_copy_of(src, dst, ss, rs, xo, b, j, src_split):
        start = pl.multiple_of(b * rows + j * rc, rc)
        dest = pl.multiple_of(b * rows + j * rc - xo * own, rc)
        return pltpu.make_async_remote_copy(
            src_ref=src.at[pl.ds(start, rc)],
            dst_ref=dst.at[src_split, pl.ds(dest, rc)],
            send_sem=ss.at[b * nc + j],
            recv_sem=rs.at[src_split, dest // rc],
            device_id={"split": xo},
            device_id_type=MESH,
        )

    part_cols = cols // PARTS

    def p_copy(h, *where):
        return x_copy_of(xs.at[h], xr.at[h], xsend.at[h], xrecv.at[h], *where)

    def l_copy(*where):
        return x_copy_of(ls, lr, lsend, lrecv, *where)

    def share_of(h, core):
        return lowx.at[h, pl.ds(pl.multiple_of(core * share, share), share)]

    def g_copy(k, h):
        return pltpu.make_async_remote_copy(
            src_ref=share_of(h, sub),
            dst_ref=share_of(h, sub),
            send_sem=gsend.at[k - 1],
            recv_sem=grecv.at[h],
            device_id={"blk": lax.rem(blk + k, nb)},
            device_id_type=MESH,
        )

    def f_copy(k, h, core):
        return pltpu.make_async_remote_copy(
            src_ref=share_of(h, core),
            dst_ref=share_of(h, core),
            send_sem=fsend.at[k - 1, h],
            recv_sem=frecv.at[k - 1, h],
            device_id={"sub": lax.rem(sub + k, nu)},
            device_id_type=MESH,
        )

    def place(i):
        d, j, side = i // (2 * nc), i // 2 % nc, i % 2
        b = jnp.where(side == 0, blk - d, blk + d)
        valid = (b >= 0) & (b < nb) & ((d > 0) | (side == 0))
        return d, j, side, jnp.clip(b, 0, nb - 1), valid

    steps = 2 * nb * nc

    def arrive(i):
        d, j, side, b, valid = place(i)

        @pl.when(valid & (d > 0) & (i < steps))
        def _():
            z_copy(b, j, side).wait_recv()

            @pl.when((side == 0) & (blk < nb - 1))
            def _():
                z_copy(b, j, 0).start()

            @pl.when((side == 1) & (blk > 0))
            def _():
                z_copy(b, j, 1).start()

            for k in range(1, nu):
                c_copy(b, j, k, sub).start()

    def compute(i):
        d, j, side, b, valid = place(i)

        @pl.when(valid & (i >= 0) & (i < steps))
        def _():
            @pl.when(d > 0)
            def _():
                for k in range(1, nu):
                    c_copy(b, j, k, lax.rem(sub - k + nu, nu)).wait_recv()

            start = pl.multiple_of(b * rows + j * rc, rc)
            xo = (b * rows + j * rc) // own
            piece = xall[pl.ds(start, rc), :]
            for h in range(PARTS):
                here = pl.ds(h * part_cols, part_cols)
                part = jnp.dot(piece, wv[:, here], preferred_element_type=jnp.float32)

                @pl.when(xo == split)
                def _():
                    at = pl.ds(pl.multiple_of(b * rows + j * rc - xo * own, rc), rc)
                    acc[at, here] = part

                @pl.when(xo != split)
                def _():
                    xs[h, pl.ds(start, rc), :] = part.astype(xs.dtype)
                    p_copy(h, xo, b, j, split).start()

    @pl.loop(0, steps + 2)
    def _(i):
        arrive(i)
        compute(i - 2)

    @pl.when(in_middle)
    def _():
        for load in bank_loads:
            load.wait()
        for p in range(group):
            @pl.when(p != blk % group)
            def _():
                for e in range(banks):
                    b_copy(e, p).wait_recv()

        @pl.loop(0, nb * nc)
        def _(n):
            b, j = n // nc, n % nc
            start = pl.multiple_of(n * rc, rc)
            xo = (n * rc) // own
            low = lax.dot_general(
                xall[pl.ds(start, rc), :], dnp[...], (((1,), (1,)), ((), ())),
                preferred_element_type=jnp.float32,
            )

            @pl.when(xo == split)
            def _():
                lacc[pl.ds(pl.multiple_of(n * rc - xo * own, rc), rc), :] = low

            @pl.when(xo != split)
            def _():
                ls[pl.ds(start, rc), :] = low
                l_copy(xo, b, j, split).start()

        @pl.loop(0, own // rc)
        def _(o):
            at = pl.ds(pl.multiple_of(o * rc, rc), rc)
            n = split * (own // rc) + o
            low = lacc[at, :]
            for k in range(1, ns):
                src = lax.rem(split + k, ns)
                l_copy(split, n // nc, n % nc, src).wait_recv()
                low = low + lr[src, at, :]
            scale = mtab[pl.ds(pl.multiple_of(n * rc, rc), rc), :]
            lowx[upper, at, :] = (low * scale).astype(lowx.dtype)

        for k in range(1, nb):
            g_copy(k, upper).start()

    def from_far(h):
        return jnp.logical_not(in_middle & (upper == h))

    for h in range(2):
        @pl.when(from_far(h))
        def _():
            g_copy(1, h).wait_recv()
            for k in range(1, nu):
                f_copy(k, h, sub).start()
    for h in range(2):
        @pl.when(from_far(h))
        def _():
            for k in range(1, nu):
                f_copy(k, h, lax.rem(sub - k + nu, nu)).wait_recv()

    for k in range(1, ns):
        for e in range(up_banks):
            u_copy(k, e, lax.rem(split - k + ns, ns)).wait_recv()

    @pl.loop(0, own // rc)
    def _(n):
        per = min(nc, own // rc)
        o = jnp.where(upper == 0, n, (own // rc // per - 1 - n // per) * per + n % per)
        at = pl.ds(pl.multiple_of(o * rc, rc), rc)
        value = rv[at, :].astype(jnp.float32) + acc[at, :]
        for h in range(2):
            value = value + jnp.dot(
                lowx[h, at, :], upp[h * wide:(h + 1) * wide, :],
                preferred_element_type=jnp.float32,
            )
        for k in range(1, ns):
            src = lax.rem(split + k, ns)
            n_all = split * (own // rc) + o
            theirs = []
            for h in range(PARTS):
                p_copy(h, split, n_all // nc, n_all % nc, src).wait_recv()
                theirs.append(xr[h, src, at, :].astype(jnp.float32))
            value = value + jnp.concatenate(theirs, axis=1)
        o_ref[at, :] = value.astype(o_ref.dtype)

    for k in range(1, ns):
        for e in range(up_banks):
            u_copy(k, e, split).wait_send()

    @pl.when(in_middle)
    def _():
        for k in range(1, nb):
            g_copy(k, upper).wait_send()

    @pl.when(jnp.logical_not(in_middle))
    def _():
        for e in range(banks):
            b_copy(e, blk % group).wait_send()

    for h in range(2):
        @pl.when(from_far(h))
        def _():
            for k in range(1, nu):
                f_copy(k, h, sub).wait_send()

    @pl.loop(0, nb * nc)
    def _(n):
        b, j = n // nc, n % nc
        xo = (b * rows + j * rc) // own

        @pl.when(xo != split)
        def _():
            for h in range(PARTS):
                p_copy(h, xo, b, j, split).wait_send()

            @pl.when(in_middle)
            def _():
                l_copy(xo, b, j, split).wait_send()

        @pl.when((b <= blk) & (blk < nb - 1))
        def _():
            z_copy(b, j, 0).wait_send()

        @pl.when((b >= blk) & (blk > 0))
        def _():
            z_copy(b, j, 1).wait_send()

        @pl.when(b != blk)
        def _():
            for k in range(1, nu):
                c_copy(b, j, k, sub).wait_send()


def shards(
    nb, ns, nu,
    attention_output_rows,
    residual,
    output_projection_weight,
    down_adapter_bank,
    up_adapter_bank,
    rollout_row_tenant,
    tenant_bank_entry,
    tenant_live_rank,
):
    rows, feats = attention_output_rows.shape
    own, cols = residual.shape
    banks, rank, _ = down_adapter_bank.shape
    up_banks = up_adapter_bank.shape[0]
    total = rollout_row_tenant.shape[0]
    wide = nb // 2 * banks * rank
    rc = CHUNK_ROWS
    chunks = total // rc
    dma = pltpu.SemaphoreType.DMA
    bf16, f32 = jnp.bfloat16, jnp.float32
    any_spec = pl.BlockSpec(memory_space=pl.ANY)
    smem = pl.BlockSpec(memory_space=pltpu.SMEM)
    vmem = pl.BlockSpec(memory_space=pltpu.VMEM)
    return pl.pallas_call(
        functools.partial(kernel, nb, ns, nu, rc),
        out_shape=jax.ShapeDtypeStruct((own, cols), bf16),
        in_specs=[smem, smem] + [any_spec] * 5 + [vmem],
        out_specs=vmem,
        scratch_shapes=[
            pltpu.VMEM((total, feats), bf16),
            pltpu.VMEM((feats, cols), bf16),
            pltpu.VMEM((own, cols), bf16),
            pltpu.VMEM((wide, feats), bf16),
            pltpu.VMEM((2 * wide, cols), bf16),
            pltpu.VMEM((total, wide), f32),
            pltpu.VMEM((own, cols), f32),
            pltpu.VMEM((own, wide), f32),
            pltpu.VMEM((PARTS, total, cols // PARTS), bf16),
            pltpu.VMEM((total, wide), f32),
            pltpu.VMEM((PARTS, ns, own, cols // PARTS), bf16),
            pltpu.VMEM((ns, own, wide), f32),
            pltpu.VMEM((2, own, wide), bf16),
            dma((2 + banks + up_banks,)),
            dma,
            dma((2, chunks)),
            dma((chunks,)),
            dma((nu - 1, chunks)),
            dma((nu - 1, chunks)),
            dma((ns - 1, up_banks)),
            dma((ns - 1, up_banks)),
            dma((PARTS, chunks)),
            dma((PARTS, ns, own // rc)),
            dma((chunks,)),
            dma((ns, own // rc)),
            dma((nb - 1,)),
            dma((2,)),
            dma((nu - 1, 2)),
            dma((nu - 1, 2)),
            dma((banks,)),
            dma((nb // 2, banks)),
        ],
        compiler_params=pltpu.CompilerParams(
            collective_id=0, has_side_effects=True
        ),
    )(
        tenant_bank_entry,
        tenant_live_rank,
        attention_output_rows,
        residual,
        output_projection_weight,
        down_adapter_bank,
        up_adapter_bank,
        rollout_row_tenant.reshape(1, total),
    )


def solution(mesh):
    in_specs = (
        P(("groups", "blk"), "split"),
        P(("groups", "split"), ("blk", "sub")),
        P("split", ("blk", "sub")),
        P("blk", None, "split"),
        P("split", None, ("blk", "sub")),
        P("groups"),
        P(),
        P(),
    )
    out_specs = P(("groups", "split"), ("blk", "sub"))
    body = functools.partial(
        shards, mesh.shape["blk"], mesh.shape["split"], mesh.shape["sub"]
    )
    return jax.shard_map(body, mesh=mesh, in_specs=in_specs, out_specs=out_specs, check_vma=False)
```
